32 devices in a mesh: blk: 8 (over z, y), col: 4 (over x, core).
Axes of the slice: x: 2, y: 2, z: 4, core: 2. Of those that a mesh axis runs over, the one named last changes fastest.
Arguments:
- amplitudes: float32 [800, 32, 1601], P('col', 'blk'), may hold values from -6 to 6
- integrals: float32 [2, 1024, 20, 1601], P(None, 'blk', 'col'), may hold values from -0.03125 to 0.03125
- block_ids: int32 [20], replicated, may hold values from 0 to 799, as said below
- mirror: int32 [16], replicated, may hold values from 0 to 15, each once
Outputs:
- ladder_residual: float32 [16, 1024], P('col', 'blk')
The draws below stay inside these ranges and needn't reach their ends.
Inputs may be any that keep to these rules, and one draw needn't show every extreme that they name: `block_ids`: 20 distinct folded block numbers; 0 and 799 are always among them. `mirror`: a permutation of the slab positions.
All inputs are finite; a program needn't handle non-finite values.
Results may differ from the reference program's by a relative error of at most 0.000073.
Values sent between devices are 32-bit elements; how exact they have to be, the bound alone decides.
A program may use at most 64 MiB of HBM per device.

```python
import jax
import jax.numpy as jnp
from jax import lax

NPAIR = 16
L = 1601
H = 800
AB = 1024
NB = 20


def draw_block_ids(key, part):
    inner = jax.random.permutation(key, H - 2)[:NB - 2] + 1
    chosen = jnp.concatenate([jnp.array([0, H - 1], jnp.int32), inner.astype(jnp.int32)])
    shuffle = jax.random.permutation(jax.random.fold_in(key, 7), NB)
    return chosen[shuffle]


def shard_levels(own_key, dims, split, low, high):
    def one(position, blocks):
        heights = jax.random.uniform(jax.random.fold_in(jax.random.fold_in(own_key, 6), position), (blocks,), jnp.float32, low / len(split), high / len(split))
        return jnp.repeat(jnp.exp(heights), dims[position] // blocks).reshape((-1,) + (1,) * (len(dims) - position - 1))

    gain = one(*split[0])
    for cut in split[1:]:
        gain = gain * one(*cut)
    return gain


def scatter_about(stream_key, dims, deviation, bound, cuts=(), held_as=jnp.bfloat16):
    loudness = shard_levels(stream_key, dims, cuts, -0.22, 0.18) if cuts else 1.0
    entries = jax.random.normal(stream_key, dims, jnp.float32) * deviation * loudness
    return jnp.minimum(jnp.maximum(entries, -bound), bound).astype(held_as)


def setup_inputs(seed: int = 0) -> dict:
    arg_keys = jax.random.split(jax.random.key(seed), 5)
    amplitudes = scatter_about(arg_keys[0], (H, 2 * NPAIR, L), 1.0, 6.0, ((0, 4), (1, 8)), jnp.float32)
    integrals = scatter_about(arg_keys[1], (2, AB, NB, L), (NB * L) ** -0.5, 0.03125, ((1, 8), (2, 4)), jnp.float32)
    block_ids = draw_block_ids(jax.random.fold_in(arg_keys[4], 71), 0)
    mirror = jax.random.permutation(arg_keys[3], NPAIR).astype(jnp.int32)
    return {"amplitudes": amplitudes, "integrals": integrals, "block_ids": block_ids, "mirror": mirror}


def reference(amplitudes, integrals, block_ids, mirror):
    selected = jnp.take(amplitudes, block_ids, axis=0)
    plus_part = jnp.einsum("krl,akl->ra", selected, integrals[0], precision=lax.Precision.HIGHEST)
    minus_part = jnp.einsum("krl,akl->ra", selected, integrals[1], precision=lax.Precision.HIGHEST)
    pair_count = plus_part.shape[0] // 2
    direct = 0.5 * (plus_part[:pair_count] + minus_part[:pair_count] + plus_part[pair_count:] - minus_part[pair_count:])
    swapped = 0.5 * (plus_part[:pair_count] - minus_part[:pair_count] + plus_part[pair_count:] + minus_part[pair_count:])
    return direct + jnp.take(swapped, mirror, axis=0)
```

```python
import functools
from contextlib import nullcontext as scope

import jax
import jax.numpy as jnp
from jax import lax
from jax.experimental import pallas as pl
from jax.experimental.pallas import tpu as pltpu
from jax.sharding import PartitionSpec as P

MESH = pl.DeviceIdType.MESH


def kernel(
    nblk, ncol,
    amp_hbm, int_hbm, ids_hbm, mirror_hbm, out_ref,
    amp_v, int_v, hi, lo, core_out, core_in, sendb, landed, gath, feed, res, swp, osend, orecv, ids, mirror,
    amp_sem, int_sem, tab_sem, cs, cr, xs, xr, zs, ys, gz, gy, os_, or_,
):
    blocks_here, rows, width = amp_v.shape
    own, _, ab = int_v.shape
    padded = hi.shape[1]
    group = feed.shape[0]
    own_pairs = osend.shape[1]
    nhi = nblk // 2
    nx = ncol // 2
    b = lax.axis_index("blk")
    c = lax.axis_index("col")
    z = b // 2
    y = b % 2
    x = c // 2
    q = c % 2
    line = nhi == 4
    pair = z + 1 - 2 * (z % 2)
    facing = nhi - 1 - z
    cross = facing + 1 - 2 * (facing % 2)
    end = jnp.logical_or(z == 0, z == nhi - 1)
    inner = jnp.logical_not(end)
    if line:
        order = (z, jnp.where(end, pair, facing), jnp.where(end, cross, pair), jnp.where(end, facing, cross))
        detour = range(own - 0, own)
    else:
        order = tuple((z + nhi - d) % nhi for d in range(nhi))
        detour = ()

    ids_copy = pltpu.make_async_copy(ids_hbm, ids, tab_sem.at[0])
    mirror_copy = pltpu.make_async_copy(mirror_hbm, mirror, tab_sem.at[1])
    ids_copy.start()
    for i in range(4):
        low, high = blocks_here * i // 4, blocks_here * (i + 1) // 4
        pltpu.make_async_copy(amp_hbm.at[low:high], amp_v.at[low:high], amp_sem.at[0]).start()
    mirror_copy.start()
    barrier = pltpu.get_barrier_semaphore()

    def greet(target):
        pl.semaphore_signal(barrier, inc=1, device_id=target, device_id_type=MESH)

    with scope("barw"):
        for j in range(1, ncol):
            greet((b, (c + j) % ncol))
        greet((z * 2 + 1 - y, c))
        if line:
            greet((pair * 2 + y, c))

            @pl.when(inner)
            def _():
                greet((facing * 2 + y, c))

            @pl.when(z == 1)
            def _():
                greet((3 * 2 + y, c))

            pl.semaphore_wait(barrier, ncol + 2 - (z == 0).astype(jnp.int32))
        else:
            for d in range(1, nhi):
                greet((order[d] * 2 + y, c))
            pl.semaphore_wait(barrier, ncol + nhi - 1)

    def core_copy(k, i):
        return pltpu.make_async_remote_copy(
            src_ref=core_out.at[k, i], dst_ref=core_in.at[k, i],
            send_sem=cs.at[0], recv_sem=cr.at[k],
            device_id=(b, x * 2 + 1 - q), device_id_type=MESH)

    def xcopy(k, i):
        return pltpu.make_async_remote_copy(
            src_ref=sendb.at[k, i - 1], dst_ref=landed.at[k, i - 1],
            send_sem=xs.at[0], recv_sem=xr.at[k, i - 1],
            device_id=(b, (x + i) % nx * 2 + q), device_id_type=MESH)

    def gcopy(k, yy, zz, send, recv, target):
        return pltpu.make_async_remote_copy(
            src_ref=gath.at[k, yy, zz], dst_ref=gath.at[k, yy, zz],
            send_sem=send, recv_sem=recv,
            device_id=(target, c), device_id_type=MESH)

    def across(k, zz):
        early = k in detour and zz is z
        return gcopy(k, y, zz, ys.at[0], gz.at[k, z] if early else gy.at[k], z * 2 + 1 - y)

    def hop(k, zsrc, zdst):
        return gcopy(k, y, zsrc, zs.at[0], gz.at[k, zsrc], zdst * 2 + y)

    def around(k):
        return gcopy(k, 1 - y, z, zs.at[0], gy.at[k], pair * 2 + y)

    def many(count, send, recv):
        piece = gath.reshape(own * nblk, rows, width).at[0:count]
        return pltpu.make_async_remote_copy(
            src_ref=piece, dst_ref=piece, send_sem=send, recv_sem=recv,
            device_id=(z * 2 + 1 - y, c), device_id_type=MESH)

    base = c * blocks_here

    def wanted(k, dest):
        here = ids[dest * own + k] - base
        ok = jnp.logical_and(here >= 0, here < blocks_here)
        at = jnp.minimum(jnp.maximum(here, 0), blocks_here - 1)
        return jnp.where(ok, amp_v[at], 0.0)

    with scope("ampw"):
        ids_copy.wait()
        pltpu.make_async_copy(amp_hbm, amp_v, amp_sem.at[0]).wait()
    int_copies = {}
    for k in range(own):
        cp = pltpu.make_async_copy(int_hbm.at[k], int_v.at[k].reshape(width, 2, ab), int_sem.at[k])
        cp.start()
        int_copies[k] = cp

    for k in range(own):
        for i in [*range(1, nx), 0]:
            core_out[k, i] = wanted(k, (x + i) % nx * 2 + 1 - q)
            core_copy(k, i).start()
    tail = (width // 128) * 128
    if padded > width:
        feed[:, tail:] = jnp.zeros((group, padded - tail), jnp.float32)

    def convert(k):
        int_copies[k].wait()
        whole = width // 16

        def split(at, count):
            for w in range(2):
                v = int_v[k, pl.ds(at * 2 + w, count, stride=2), :]
                h = v.astype(jnp.bfloat16)
                l = (v - h.astype(jnp.float32)).astype(jnp.bfloat16)
                if count < 16:
                    blank = jnp.zeros((16 - count, ab), jnp.bfloat16)
                    h = jnp.concatenate([h, blank], axis=0)
                    l = jnp.concatenate([l, blank], axis=0)
                hi[k, pl.ds(at, 16), w * ab:(w + 1) * ab] = h
                lo[k, pl.ds(at, 16), w * ab:(w + 1) * ab] = l

        def strip(i, carry):
            split(pl.multiple_of(i * 16, 16), 16)
            return carry

        lax.fori_loop(0, whole, strip, 0, unroll=4)
        done = whole * 16
        if width > done:
            split(done, width - done)
            done += 16
        if padded > done:
            hi[k, done:] = jnp.zeros((padded - done, 2 * ab), jnp.bfloat16)
            lo[k, done:] = jnp.zeros((padded - done, 2 * ab), jnp.bfloat16)

    @pl.when(q == 1)
    def _():
        for k in range(2):
            convert(k)

    for k in range(own):
        with scope(f"x{k}"):
            mine = [wanted(k, (x + i) % nx * 2 + q) for i in range(1, nx)]
            pltpu.make_async_remote_copy(
                src_ref=core_out.at[k], dst_ref=core_in.at[k], send_sem=cs.at[0], recv_sem=cr.at[k],
                device_id=(b, x * 2 + 1 - q), device_id_type=MESH).wait_recv()
            for i in range(1, nx):
                sendb[k, i - 1] = mine[i - 1] + core_in[k, i]
                xcopy(k, i).start()

    def own_piece(k):
        total = wanted(k, c) + core_in[k, 0]
        for i in range(1, nx):
            xcopy(k, i).wait_recv()
            total = total + landed[k, i - 1]
        gath[k, y, z] = total
        if line:
            @pl.when(z == 3)
            def _():
                hop(k, z, 1).start()

            @pl.when(inner)
            def _():
                hop(k, z, facing).start()

            hop(k, z, pair).start()
        else:
            for d in range(1, nhi):
                hop(k, z, (z + d) % nhi).start()
        across(k, z).start()

    def relay(k, d):
        zz = order[d]
        hop(k, zz, z).wait_recv()
        if not line:
            across(k, zz).start()
            return
        if d != 2:
            @pl.when(inner)
            def _():
                hop(k, zz, pair).start()
        else:
            @pl.when(z == 1)
            def _():
                hop(k, zz, facing).start()

        if k in detour and d < 3:
            @pl.when(end if d == 2 else inner)
            def _():
                across(k, zz).start()
        else:
            across(k, zz).start()

    def pass_on(where):
        if line:
            @pl.when(where)
            def _():
                for k in detour:
                    gcopy(k, 1 - y, z, ys.at[0], gz.at[k, z], z * 2 + 1 - y).wait_recv()
                    around(k).start()

    def multiply(k, yy, acc):
        for zz in range(nhi):
            feed[zz * rows:(zz + 1) * rows, :width] = gath[k, yy, zz]
        f = feed[...]
        fh = f.astype(jnp.bfloat16)
        fl = (f - fh.astype(jnp.float32)).astype(jnp.bfloat16)
        both = jnp.concatenate([fh, fl], axis=0)
        big = jnp.dot(both, hi[k], preferred_element_type=jnp.float32)
        small = jnp.dot(fh, lo[k], preferred_element_type=jnp.float32)
        part = big[:group] + (big[group:] + small)
        return part if acc is None else acc + part

    acc = other = None
    ready = 2
    with scope("cb"):
        @pl.when(q == 0)
        def _():
            for k in range(2):
                convert(k)

        for k in range(2, ready):
            convert(k)
    for d in range(nhi):
        if d == nhi - 1:
            with scope("fe"):
                pass_on(end)
        for k in range(own):
            with scope(f"r{d}_{k}"):
                if d == 0:
                    own_piece(k)
                else:
                    relay(k, d)
            if ready < own and (d > 0 or k == own - 1):
                with scope(f"conv{ready}"):
                    convert(ready)
                ready += 1
            if d == nhi - 1:
                with scope(f"p{k}"):
                    acc = multiply(k, y, acc)
    with scope("fi"):
        pass_on(inner)
    with scope("sends"):
        mirror_copy.wait()
        pltpu.make_async_remote_copy(
            src_ref=core_out, dst_ref=core_in, send_sem=cs.at[0], recv_sem=cr.at[0],
            device_id=(b, x * 2 + 1 - q), device_id_type=MESH).wait_send()
        pltpu.make_async_remote_copy(
            src_ref=sendb, dst_ref=landed, send_sem=xs.at[0], recv_sem=xr.at[0, 0],
            device_id=(b, (x + 1) % nx * 2 + q), device_id_type=MESH).wait_send()
    for k in range(own):
        with scope(f"w{k}"):
            many(nhi - (1 if k in detour else 0), ys.at[0], gy.at[k]).wait_recv()
        with scope(f"q{k}"):
            other = multiply(k, 1 - y, other)

    res[y] = acc
    res[1 - y] = other
    deep = group // 2
    for yy in range(2):
        first = res[yy, :deep]
        second = res[yy, deep:]
        sums = first[:, :ab] + second[:, :ab]
        diffs = first[:, ab:] - second[:, ab:]
        swapped = 0.5 * (sums - diffs)
        direct = 0.5 * (sums + diffs)
        for zz in range(nhi // 2):
            at = (zz * 2 + yy) * rows
            swp[0, at:at + rows] = direct[zz * rows:(zz + 1) * rows]
            swp[1, at:at + rows] = swapped[zz * rows:(zz + 1) * rows]
    for g in range(ncol):
        for i in range(own_pairs):
            p = g * own_pairs + i
            osend[g, i:i + 1, :] = swp[0, p:p + 1] + swp[1, pl.ds(mirror[p], 1), :]

    def ocopy(j):
        return pltpu.make_async_remote_copy(
            src_ref=osend.at[(c + j) % ncol], dst_ref=orecv.at[j - 1],
            send_sem=os_.at[0], recv_sem=or_.at[0],
            device_id=(b, (c + j) % ncol), device_id_type=MESH)

    for j in range(1, ncol):
        ocopy(j).start()
    with scope("sends2"):
        many(own * nhi - len(detour), ys.at[0], gy.at[0]).wait_send()
        if line:
            for layer, count in ((0, own), (1, 5 * own), (2, 4 * own), (3, 2 * own)):
                @pl.when(z == layer)
                def _():
                    many(count + len(detour), zs.at[0], gy.at[0]).wait_send()
        else:
            many(own * (nhi - 1), zs.at[0], gy.at[0]).wait_send()
    total = osend[c]
    with scope("owait"):
        every = pltpu.make_async_remote_copy(
            src_ref=orecv, dst_ref=orecv, send_sem=os_.at[0], recv_sem=or_.at[0],
            device_id=(b, (c + 1) % ncol), device_id_type=MESH)
        every.wait_recv()
    for j in range(1, ncol):
        total = total + orecv[j - 1]
    out_ref[...] = total
    every.wait_send()


def body(nblk, ncol, amplitudes, integrals, block_ids, mirror):
    blocks_here, rows, width = amplitudes.shape
    _, ab, own, _ = integrals.shape
    pairs = mirror.shape[0]
    own_pairs = pairs // ncol
    padded = -(-width // 128) * 128
    nhi = nblk // 2
    nx = ncol // 2
    f32 = jnp.float32
    dma = pltpu.SemaphoreType.DMA
    return pl.pallas_call(
        functools.partial(kernel, nblk, ncol),
        out_shape=pltpu.VMEM((own_pairs, ab), f32),
        in_specs=[pl.BlockSpec(memory_space=pl.ANY)] * 4,
        out_specs=pl.BlockSpec(memory_space=pltpu.VMEM),
        scratch_shapes=[
            pltpu.VMEM((blocks_here, rows, width), f32),
            pltpu.VMEM((own, 2 * width, ab), f32),
            pltpu.VMEM((own, padded, 2 * ab), jnp.bfloat16),
            pltpu.VMEM((own, padded, 2 * ab), jnp.bfloat16),
            pltpu.VMEM((own, nx, rows, width), f32),
            pltpu.VMEM((own, nx, rows, width), f32),
            pltpu.VMEM((own, nx - 1, rows, width), f32),
            pltpu.VMEM((own, nx - 1, rows, width), f32),
            pltpu.VMEM((own, 2, nhi, rows, width), f32),
            pltpu.VMEM((nhi * rows, padded), f32),
            pltpu.VMEM((2, nhi * rows, 2 * ab), f32),
            pltpu.VMEM((2, pairs, ab), f32),
            pltpu.VMEM((ncol, own_pairs, ab), f32),
            pltpu.VMEM((ncol - 1, own_pairs, ab), f32),
            pltpu.SMEM(block_ids.shape, jnp.int32),
            pltpu.SMEM(mirror.shape, jnp.int32),
            dma((1,)),
            dma((own,)),
            dma((2,)),
            dma((1,)),
            dma((own,)),
            dma((1,)),
            dma((own, nx - 1)),
            dma((1,)),
            dma((1,)),
            dma((own, nhi)),
            dma((own,)),
            dma((1,)),
            dma((1,)),
        ],
        compiler_params=pltpu.CompilerParams(
            collective_id=0, has_side_effects=True, vmem_limit_bytes=60 * 1024 * 1024
        ),
    )(amplitudes, jnp.transpose(integrals, (2, 3, 0, 1)), block_ids, mirror)


def solution(mesh):
    in_specs = (P("col", "blk", None), P(None, "blk", "col", None), P(), P())
    out_specs = P("col", "blk")
    call = functools.partial(body, mesh.shape["blk"], mesh.shape["col"])
    return jax.shard_map(call, mesh=mesh, in_specs=in_specs, out_specs=out_specs, check_vma=False)
```

```python
import functools
from contextlib import nullcontext as scope

import jax
import jax.numpy as jnp
from jax import lax
from jax.experimental import pallas as pl
from jax.experimental.pallas import tpu as pltpu
from jax.sharding import PartitionSpec as P

MESH = pl.DeviceIdType.MESH


def kernel(
    nblk, ncol,
    amp_hbm, int_hbm, ids_hbm, mirror_hbm, out_ref,
    amp_v, int_v, hi, lo, core_out, core_in, sendb, landed, gath, feed, swp, osend, orecv, ids, mirror,
    amp_sem, int_sem, tab_sem, cs, cr, xs, xr, zs, ys, gz, gd, gy, os_, or_,
):
    blocks_here, rows, width = amp_hbm.shape
    own, _, ab = int_v.shape
    spans = chunks(width)
    parts = range(len(spans))
    last = parts[-1]
    padded = hi.shape[1]
    group = feed.shape[0]
    own_pairs = osend.shape[1]
    nhi = nblk // 2
    nx = ncol // 2
    b = lax.axis_index("blk")
    c = lax.axis_index("col")
    z = b // 2
    y = b % 2
    x = c // 2
    q = c % 2
    line = nhi == 4
    pair = z + 1 - 2 * (z % 2)
    facing = nhi - 1 - z
    cross = facing + 1 - 2 * (facing % 2)
    end = jnp.logical_or(z == 0, z == nhi - 1)
    inner = jnp.logical_not(end)
    if line:
        order = (z, jnp.where(end, pair, facing), jnp.where(end, cross, pair), jnp.where(end, facing, cross))
        detour = ()
    else:
        order = tuple((z + nhi - d) % nhi for d in range(nhi))
        detour = ()

    ids_copy = pltpu.make_async_copy(ids_hbm, ids, tab_sem.at[0])
    mirror_copy = pltpu.make_async_copy(mirror_hbm, mirror, tab_sem.at[1])
    ids_copy.start()
    amp_copies = []
    for h in parts:
        for i in range(4):
            at = pl.ds(blocks_here * i // 4, blocks_here * (i + 1) // 4 - blocks_here * i // 4)
            pltpu.make_async_copy(amp_hbm.at[at, :, spans[h]], amp_v[h].at[at], amp_sem.at[h]).start()
        amp_copies.append(pltpu.make_async_copy(amp_hbm.at[:, :, spans[h]], amp_v[h], amp_sem.at[h]))
    mirror_copy.start()
    barrier = pltpu.get_barrier_semaphore()

    def greet(target):
        pl.semaphore_signal(barrier, inc=1, device_id=target, device_id_type=MESH)

    with scope("barw"):
        for j in range(1, ncol):
            greet((b, (c + j) % ncol))
        greet((z * 2 + 1 - y, c))
        if line:
            greet((pair * 2 + y, c))

            @pl.when(inner)
            def _():
                greet((facing * 2 + y, c))

            @pl.when(z == 1)
            def _():
                greet((3 * 2 + y, c))

            pl.semaphore_wait(barrier, ncol + 2 - (z == 0).astype(jnp.int32))
        else:
            for d in range(1, nhi):
                greet((order[d] * 2 + y, c))
            pl.semaphore_wait(barrier, ncol + nhi - 1)

    def core_copy(k, i, h):
        return pltpu.make_async_remote_copy(
            src_ref=core_out.at[k, i, :, spans[h]], dst_ref=core_in.at[k, i, :, spans[h]],
            send_sem=cs.at[h], recv_sem=cr.at[h],
            device_id=(b, x * 2 + 1 - q), device_id_type=MESH)

    def core_all(h):
        return pltpu.make_async_remote_copy(
            src_ref=core_out.at[:, :, :, spans[h]], dst_ref=core_in.at[:, :, :, spans[h]],
            send_sem=cs.at[h], recv_sem=cr.at[h],
            device_id=(b, x * 2 + 1 - q), device_id_type=MESH)

    def xcopy(k, i, h):
        return pltpu.make_async_remote_copy(
            src_ref=sendb.at[k, i - 1, :, spans[h]], dst_ref=landed.at[k, i - 1, :, spans[h]],
            send_sem=xs.at[h], recv_sem=xr.at[h, k, i - 1],
            device_id=(b, (x + i) % nx * 2 + 1 - q), device_id_type=MESH)

    def gcopy(k, h, yy, zz, send, recv, target):
        piece = gath.at[k, yy, zz, :, spans[h]]
        return pltpu.make_async_remote_copy(
            src_ref=piece, dst_ref=piece, send_sem=send, recv_sem=recv,
            device_id=(target, c), device_id_type=MESH)

    def fill(k, h):
        return gy.at[h, k]

    def across(k, h, zz):
        early = (k, h) in detour and zz is z
        recv = gd.at[detour.index((k, h))] if early else fill(k, h)
        return gcopy(k, h, y, zz, ys.at[h], recv, z * 2 + 1 - y)

    def hop(k, h, zsrc, zdst):
        return gcopy(k, h, y, zsrc, zs.at[h], gz.at[h, k, (zsrc + nhi - zdst) % nhi - 1], zdst * 2 + y)

    def around(k, h):
        return gcopy(k, h, 1 - y, z, zs.at[h], fill(k, h), pair * 2 + y)

    def many(count, h, send, recv):
        piece = gath.reshape(own * nblk, rows, width).at[0:count, :, spans[h]]
        return pltpu.make_async_remote_copy(
            src_ref=piece, dst_ref=piece, send_sem=send, recv_sem=recv,
            device_id=(z * 2 + 1 - y, c), device_id_type=MESH)

    base = c * blocks_here

    def wanted(k, dest, h):
        here = ids[dest * own + k] - base
        ok = jnp.logical_and(here >= 0, here < blocks_here)
        at = jnp.minimum(jnp.maximum(here, 0), blocks_here - 1)
        return jnp.where(ok, amp_v[h][at], 0.0)

    def to_core(h):
        with scope(f"amp{h}"):
            amp_copies[h].wait()
        for k in range(own):
            for i in [*range(1, nx), 0]:
                dest = (x + i) % nx * 2 + q if i else x * 2 + 1 - q
                core_out[k, i, :, spans[h]] = wanted(k, dest, h)
                core_copy(k, i, h).start()

    def over_x(h):
        with scope(f"x{h}"):
            core_all(h).wait_recv()
            for k in range(own):
                for i in range(1, nx):
                    mine = wanted(k, (x + i) % nx * 2 + 1 - q, h)
                    sendb[k, i - 1, :, spans[h]] = mine + core_in[k, i, :, spans[h]]
                    xcopy(k, i, h).start()

    ids_copy.wait()
    to_core(0)

    @pl.when(q == 1)
    def _():
        over_x(0)

    for h in parts[1:]:
        to_core(h)
    int_copies = {}
    for k in range(own):
        cp = pltpu.make_async_copy(int_hbm.at[k], int_v.at[k].reshape(width, 2, ab), int_sem.at[k])
        cp.start()
        int_copies[k] = cp

    @pl.when(q == 1)
    def _():
        for h in parts[1:]:
            over_x(h)
    tail = (width // 128) * 128
    if padded > width:
        feed[:, tail:] = jnp.zeros((group, padded - tail), jnp.float32)

    def convert(k):
        int_copies[k].wait()
        whole = width // 16

        def split(at, count):
            for w in range(2):
                v = int_v[k, pl.ds(at * 2 + w, count, stride=2), :]
                h = v.astype(jnp.bfloat16)
                l = (v - h.astype(jnp.float32)).astype(jnp.bfloat16)
                if count < 16:
                    blank = jnp.zeros((16 - count, ab), jnp.bfloat16)
                    h = jnp.concatenate([h, blank], axis=0)
                    l = jnp.concatenate([l, blank], axis=0)
                hi[k, pl.ds(at, 16), w * ab:(w + 1) * ab] = h
                lo[k, pl.ds(at, 16), w * ab:(w + 1) * ab] = l

        def strip(i, carry):
            split(pl.multiple_of(i * 16, 16), 16)
            return carry

        lax.fori_loop(0, whole, strip, 0, unroll=4)
        done = whole * 16
        if width > done:
            split(done, width - done)
            done += 16
        if padded > done:
            hi[k, done:] = jnp.zeros((padded - done, 2 * ab), jnp.bfloat16)
            lo[k, done:] = jnp.zeros((padded - done, 2 * ab), jnp.bfloat16)

    def own_piece(k, h):
        total = wanted(k, c, h) + core_in[k, 0, :, spans[h]]
        for i in range(1, nx):
            xcopy(k, i, h).wait_recv()
            total = total + landed[k, i - 1, :, spans[h]]
        gath[k, y, z, :, spans[h]] = total
        if line:
            @pl.when(z == 3)
            def _():
                hop(k, h, z, 1).start()

            @pl.when(inner)
            def _():
                hop(k, h, z, facing).start()

            hop(k, h, z, pair).start()
            across(k, h, z).start()
        else:
            for d in range(1, nhi):
                hop(k, h, z, (z + d) % nhi).start()
            across(k, h, z).start()

    def relay(k, h, d):
        zz = order[d]
        hop(k, h, zz, z).wait_recv()
        if not line:
            across(k, h, zz).start()
            return
        if d == 1:
            @pl.when(inner)
            def _():
                hop(k, h, zz, pair).start()
        elif d == 2:
            @pl.when(z == 1)
            def _():
                hop(k, h, zz, facing).start()
        else:
            @pl.when(inner)
            def _():
                hop(k, h, zz, pair).start()

        if (k, h) in detour and d < 3:
            @pl.when(end if d == 2 else inner)
            def _():
                across(k, h, zz).start()
        else:
            across(k, h, zz).start()

    def pass_on(j):
        k, h = detour[j]
        gcopy(k, h, 1 - y, z, ys.at[h], gd.at[j], z * 2 + 1 - y).wait_recv()
        around(k, h).start()

    def multiply(k, h, acc):
        span = slice(spans[h].start, padded if h == last else spans[h].stop)
        for yy in range(2):
            for zz in range(nhi):
                at = (yy * nhi + zz) * rows
                feed[at:at + rows, spans[h]] = gath[k, yy, zz, :, spans[h]]
        f = feed[:, span]
        fh = f.astype(jnp.bfloat16)
        fl = (f - fh.astype(jnp.float32)).astype(jnp.bfloat16)
        both = jnp.concatenate([fh, fl], axis=0)
        big = jnp.dot(both, hi[k, span], preferred_element_type=jnp.float32)
        small = jnp.dot(fh, lo[k, span], preferred_element_type=jnp.float32)
        part = big[:group] + (big[group:] + small)
        return part if acc is None else acc + part

    @pl.when(q == 0)
    def _():
        with scope("cb"):
            for k in range(min(1, own)):
                convert(k)
        for h in parts:
            over_x(h)

    @pl.when(q == 1)
    def _():
        with scope("cb"):
            for k in range(min(2, own)):
                convert(k)


    acc = None
    for h in parts:
        for k in range(own):
            with scope(f"own{h}{k}"):
                own_piece(k, h)
    pieces = [(k, h) for h in parts for k in range(own)]
    with scope("cm"):
        for k in range(0, min(0 + 0, own)):
            convert(k)
    if line:
        @pl.when(inner)
        def _():
            steps = [(j + (0, -3, 3)[d - 1], d, j) for j in range(len(pieces)) for d in range(1, nhi)]
            steps += [(14 + i, nhi, i) for i in range(len(detour))]
            for _, d, j in sorted(steps):
                with scope(f"i{d}_{j}"):
                    if d == nhi:
                        pass_on(j)
                    else:
                        relay(*pieces[j], d)

        @pl.when(end)
        def _():
            steps = [(j, 1, j) for j in range(len(pieces))]
            steps += [(0 + i, 4, i) for i in range(len(detour))]
            for _, d, j in sorted(steps):
                with scope(f"e{d}_{j}"):
                    if d == nhi:
                        pass_on(j)
                    else:
                        relay(*pieces[j], 1)
    else:
        for k, h in pieces:
            for d in range(1, nhi):
                relay(k, h, d)
    with scope("cc"):
        for k in range(1, min(2, own)):
            @pl.when(q == 0)
            def _():
                convert(k)

        for k in range(2, own):
            convert(k)

    def product(j, acc):
        k, h = pieces[j]
        with scope(f"w{h}{k}"):
            many(nhi - ((k, h) in detour), h, ys.at[h], fill(k, h)).wait_recv()
        with scope(f"q{h}{k}"):
            return multiply(k, h, acc)

    ready = 0
    for n in range(len(pieces) + 1):
        if line:
            @pl.when(end)
            def _():
                if n < len(pieces):
                    with scope(f"e2_{n}"):
                        relay(*pieces[n], 2)
                if n >= 1:
                    with scope(f"e3_{n-1}"):
                        relay(*pieces[n - 1], 3)

        if n == 1 + 1:
            with scope("sends"):
                mirror_copy.wait()
                for h in parts:
                    core_all(h).wait_send()
                    pltpu.make_async_remote_copy(
                        src_ref=sendb.at[:, :, :, spans[h]], dst_ref=landed.at[:, :, :, spans[h]],
                        send_sem=xs.at[h], recv_sem=xr.at[h, 0, 0],
                        device_id=(b, (x + 1) % nx * 2 + q), device_id_type=MESH).wait_send()
        if n >= 1 + 5 and n < len(pieces) + 1 - 1:
            acc = product(ready, acc)
            ready += 1
    for j in range(ready, len(pieces)):
        acc = product(j, acc)

    deep = group // 4
    for yy in range(2):
        first = acc[2 * yy * deep:(2 * yy + 1) * deep]
        second = acc[(2 * yy + 1) * deep:(2 * yy + 2) * deep]
        sums = first[:, :ab] + second[:, :ab]
        diffs = first[:, ab:] - second[:, ab:]
        swapped = 0.5 * (sums - diffs)
        direct = 0.5 * (sums + diffs)
        for zz in range(nhi // 2):
            at = (zz * 2 + yy) * rows
            swp[0, at:at + rows] = direct[zz * rows:(zz + 1) * rows]
            swp[1, at:at + rows] = swapped[zz * rows:(zz + 1) * rows]
    for g in range(ncol):
        for i in range(own_pairs):
            p = g * own_pairs + i
            osend[g, i:i + 1, :] = swp[0, p:p + 1] + swp[1, pl.ds(mirror[p], 1), :]

    def ocopy(j):
        return pltpu.make_async_remote_copy(
            src_ref=osend.at[(c + j) % ncol], dst_ref=orecv.at[j - 1],
            send_sem=os_.at[0], recv_sem=or_.at[0],
            device_id=(b, (c + j) % ncol), device_id_type=MESH)

    for j in range(1, ncol):
        ocopy(j).start()
    with scope("sends2"):
        for h in parts:
            gone = len([j for j in detour if j[1] == h])
            many(own * nhi - gone, h, ys.at[h], gy.at[0, 0]).wait_send()
            if line:
                for layer, count in ((0, own), (1, 5 * own), (2, 4 * own), (3, 2 * own)):
                    @pl.when(z == layer)
                    def _():
                        many(count + gone, h, zs.at[h], gy.at[0, 0]).wait_send()
            else:
                many(own * (nhi - 1), h, zs.at[h], gy.at[0, 0]).wait_send()
    total = osend[c]
    with scope("owait"):
        every = pltpu.make_async_remote_copy(
            src_ref=orecv, dst_ref=orecv, send_sem=os_.at[0], recv_sem=or_.at[0],
            device_id=(b, (c + 1) % ncol), device_id_type=MESH)
        every.wait_recv()
    for j in range(1, ncol):
        total = total + orecv[j - 1]
    out_ref[...] = total
    every.wait_send()


def chunks(width):
    middle = width // 2 // 256 * 256
    return (slice(0, middle), slice(middle, width)) if middle else (slice(0, width),)


def body(nblk, ncol, amplitudes, integrals, block_ids, mirror):
    blocks_here, rows, width = amplitudes.shape
    _, ab, own, _ = integrals.shape
    pairs = mirror.shape[0]
    own_pairs = pairs // ncol
    padded = -(-width // 128) * 128
    nhi = nblk // 2
    nx = ncol // 2
    f32 = jnp.float32
    dma = pltpu.SemaphoreType.DMA
    parts = len(chunks(width))
    return pl.pallas_call(
        functools.partial(kernel, nblk, ncol),
        out_shape=pltpu.VMEM((own_pairs, ab), f32),
        in_specs=[pl.BlockSpec(memory_space=pl.ANY)] * 4,
        out_specs=pl.BlockSpec(memory_space=pltpu.VMEM),
        scratch_shapes=[
            tuple(pltpu.VMEM((blocks_here, rows, s.stop - s.start), f32) for s in chunks(width)),
            pltpu.VMEM((own, 2 * width, ab), f32),
            pltpu.VMEM((own, padded, 2 * ab), jnp.bfloat16),
            pltpu.VMEM((own, padded, 2 * ab), jnp.bfloat16),
            pltpu.VMEM((own, nx, rows, width), f32),
            pltpu.VMEM((own, nx, rows, width), f32),
            pltpu.VMEM((own, nx - 1, rows, width), f32),
            pltpu.VMEM((own, nx - 1, rows, width), f32),
            pltpu.VMEM((own, 2, nhi, rows, width), f32),
            pltpu.VMEM((2 * nhi * rows, padded), f32),
            pltpu.VMEM((2, pairs, ab), f32),
            pltpu.VMEM((ncol, own_pairs, ab), f32),
            pltpu.VMEM((ncol - 1, own_pairs, ab), f32),
            pltpu.SMEM(block_ids.shape, jnp.int32),
            pltpu.SMEM(mirror.shape, jnp.int32),
            dma((parts,)),
            dma((own,)),
            dma((2,)),
            dma((parts,)),
            dma((parts,)),
            dma((parts,)),
            dma((parts, own, nx - 1)),
            dma((parts,)),
            dma((parts,)),
            dma((parts, own, nhi - 1)),
            dma((1,)),
            dma((parts, own)),
            dma((1,)),
            dma((1,)),
        ],
        compiler_params=pltpu.CompilerParams(
            collective_id=0, has_side_effects=True, vmem_limit_bytes=60 * 1024 * 1024
        ),
    )(amplitudes, jnp.transpose(integrals, (2, 3, 0, 1)), block_ids, mirror)


def solution(mesh):
    in_specs = (P("col", "blk", None), P(None, "blk", "col", None), P(), P())
    out_specs = P("col", "blk")
    call = functools.partial(body, mesh.shape["blk"], mesh.shape["col"])
    return jax.shard_map(call, mesh=mesh, in_specs=in_specs, out_specs=out_specs, check_vma=False)
```

```python
import functools
from contextlib import nullcontext as scope

import jax
import jax.numpy as jnp
from jax import lax
from jax.experimental import pallas as pl
from jax.experimental.pallas import tpu as pltpu
from jax.sharding import PartitionSpec as P

MESH = pl.DeviceIdType.MESH


def kernel(
    nblk, ncol,
    amp_hbm, int_hbm, ids_hbm, mirror_hbm, out_ref,
    amp_v, int_v, hi, lo, core_out, core_in, sendb, landed, gath, feed, swp, osend, orecv, ids, mirror,
    amp_sem, int_sem, tab_sem, cs, cr, xs, xr, zs, ys, gz, gd, gy, os_, or_,
):
    blocks_here, rows, width = amp_hbm.shape
    own, _, ab = int_v.shape
    spans = chunks(width)
    parts = range(len(spans))
    last = parts[-1]
    padded = hi.shape[1]
    group = feed.shape[0]
    own_pairs = osend.shape[1]
    nhi = nblk // 2
    nx = ncol // 2
    b = lax.axis_index("blk")
    c = lax.axis_index("col")
    z = b // 2
    y = b % 2
    x = c // 2
    q = c % 2
    line = nhi == 4
    pair = z + 1 - 2 * (z % 2)
    facing = nhi - 1 - z
    cross = facing + 1 - 2 * (facing % 2)
    end = jnp.logical_or(z == 0, z == nhi - 1)
    inner = jnp.logical_not(end)
    if line:
        order = (z, jnp.where(end, pair, facing), jnp.where(end, cross, pair), jnp.where(end, facing, cross))
        detour = ()
    else:
        order = tuple((z + nhi - d) % nhi for d in range(nhi))
        detour = ()

    ids_copy = pltpu.make_async_copy(ids_hbm, ids, tab_sem.at[0])
    mirror_copy = pltpu.make_async_copy(mirror_hbm, mirror, tab_sem.at[1])
    ids_copy.start()
    amp_copies = []
    for h in parts:
        for i in range(4):
            at = pl.ds(blocks_here * i // 4, blocks_here * (i + 1) // 4 - blocks_here * i // 4)
            pltpu.make_async_copy(amp_hbm.at[at, :, spans[h]], amp_v[h].at[at], amp_sem.at[h]).start()
        amp_copies.append(pltpu.make_async_copy(amp_hbm.at[:, :, spans[h]], amp_v[h], amp_sem.at[h]))
    mirror_copy.start()
    barrier = pltpu.get_barrier_semaphore()

    def greet(target):
        pl.semaphore_signal(barrier, inc=1, device_id=target, device_id_type=MESH)

    with scope("barw"):
        for j in range(1, ncol):
            greet((b, (c + j) % ncol))
        greet((z * 2 + 1 - y, c))
        if line:
            greet((pair * 2 + y, c))

            @pl.when(inner)
            def _():
                greet((facing * 2 + y, c))

            @pl.when(z == 1)
            def _():
                greet((3 * 2 + y, c))

            @pl.when(z == 0)
            def _():
                greet((2 * 2 + y, c))

            pl.semaphore_wait(barrier, ncol + 2 - (z == 0).astype(jnp.int32) + (z == 2).astype(jnp.int32))
        else:
            for d in range(1, nhi):
                greet((order[d] * 2 + y, c))
            pl.semaphore_wait(barrier, ncol + nhi - 1)

    def core_copy(k, i, h):
        return pltpu.make_async_remote_copy(
            src_ref=core_out.at[k, i, :, spans[h]], dst_ref=core_in.at[k, i, :, spans[h]],
            send_sem=cs.at[h], recv_sem=cr.at[h],
            device_id=(b, x * 2 + 1 - q), device_id_type=MESH)

    def core_all(h):
        return pltpu.make_async_remote_copy(
            src_ref=core_out.at[:, :, :, spans[h]], dst_ref=core_in.at[:, :, :, spans[h]],
            send_sem=cs.at[h], recv_sem=cr.at[h],
            device_id=(b, x * 2 + 1 - q), device_id_type=MESH)

    def xcopy(k, i, h):
        return pltpu.make_async_remote_copy(
            src_ref=sendb.at[k, i - 1, :, spans[h]], dst_ref=landed.at[k, i - 1, :, spans[h]],
            send_sem=xs.at[h], recv_sem=xr.at[h, k, i - 1],
            device_id=(b, (x + i) % nx * 2 + 1 - q), device_id_type=MESH)

    def gcopy(k, h, yy, zz, send, recv, target):
        piece = gath.at[k, yy, zz, :, spans[h]]
        return pltpu.make_async_remote_copy(
            src_ref=piece, dst_ref=piece, send_sem=send, recv_sem=recv,
            device_id=(target, c), device_id_type=MESH)

    def fill(k, h):
        return gy.at[h, k]

    def across(k, h, zz):
        early = (k, h) in detour and zz is z
        recv = gd.at[detour.index((k, h))] if early else fill(k, h)
        return gcopy(k, h, y, zz, ys.at[h], recv, z * 2 + 1 - y)

    def hop(k, h, zsrc, zdst):
        return gcopy(k, h, y, zsrc, zs.at[h], gz.at[h, k, (zsrc + nhi - zdst) % nhi - 1], zdst * 2 + y)

    def around(k, h):
        return gcopy(k, h, 1 - y, z, zs.at[h], fill(k, h), pair * 2 + y)

    def many(count, h, send, recv):
        piece = gath.reshape(own * nblk, rows, width).at[0:count, :, spans[h]]
        return pltpu.make_async_remote_copy(
            src_ref=piece, dst_ref=piece, send_sem=send, recv_sem=recv,
            device_id=(z * 2 + 1 - y, c), device_id_type=MESH)

    base = c * blocks_here

    def wanted(k, dest, h):
        here = ids[dest * own + k] - base
        ok = jnp.logical_and(here >= 0, here < blocks_here)
        at = jnp.minimum(jnp.maximum(here, 0), blocks_here - 1)
        return jnp.where(ok, amp_v[h][at], 0.0)

    def to_core(h):
        with scope(f"amp{h}"):
            amp_copies[h].wait()
        for k in range(own):
            for i in [*range(1, nx), 0]:
                dest = (x + i) % nx * 2 + q if i else x * 2 + 1 - q
                core_out[k, i, :, spans[h]] = wanted(k, dest, h)
                core_copy(k, i, h).start()

    def over_x(h):
        with scope(f"x{h}"):
            core_all(h).wait_recv()
            for k in range(own):
                for i in range(1, nx):
                    mine = wanted(k, (x + i) % nx * 2 + 1 - q, h)
                    sendb[k, i - 1, :, spans[h]] = mine + core_in[k, i, :, spans[h]]
                    xcopy(k, i, h).start()

    ids_copy.wait()
    to_core(0)

    @pl.when(q == 1)
    def _():
        over_x(0)

    for h in parts[1:]:
        to_core(h)
    int_copies = {}
    for k in range(own):
        cp = pltpu.make_async_copy(int_hbm.at[k], int_v.at[k].reshape(width, 2, ab), int_sem.at[k])
        cp.start()
        int_copies[k] = cp

    @pl.when(q == 1)
    def _():
        for h in parts[1:]:
            over_x(h)
    tail = (width // 128) * 128
    if padded > width:
        feed[:, tail:] = jnp.zeros((group, padded - tail), jnp.float32)

    def convert(k):
        int_copies[k].wait()
        whole = width // 16

        def split(at, count):
            for w in range(2):
                v = int_v[k, pl.ds(at * 2 + w, count, stride=2), :]
                h = v.astype(jnp.bfloat16)
                l = (v - h.astype(jnp.float32)).astype(jnp.bfloat16)
                if count < 16:
                    blank = jnp.zeros((16 - count, ab), jnp.bfloat16)
                    h = jnp.concatenate([h, blank], axis=0)
                    l = jnp.concatenate([l, blank], axis=0)
                hi[k, pl.ds(at, 16), w * ab:(w + 1) * ab] = h
                lo[k, pl.ds(at, 16), w * ab:(w + 1) * ab] = l

        def strip(i, carry):
            split(pl.multiple_of(i * 16, 16), 16)
            return carry

        lax.fori_loop(0, whole, strip, 0, unroll=4)
        done = whole * 16
        if width > done:
            split(done, width - done)
            done += 16
        if padded > done:
            hi[k, done:] = jnp.zeros((padded - done, 2 * ab), jnp.bfloat16)
            lo[k, done:] = jnp.zeros((padded - done, 2 * ab), jnp.bfloat16)

    def own_piece(k, h):
        total = wanted(k, c, h) + core_in[k, 0, :, spans[h]]
        for i in range(1, nx):
            xcopy(k, i, h).wait_recv()
            total = total + landed[k, i - 1, :, spans[h]]
        gath[k, y, z, :, spans[h]] = total
        if line:
            @pl.when(z == 3)
            def _():
                hop(k, h, z, 1).start()

            @pl.when(z == 2)
            def _():
                hop(k, h, z, 0).start()

            @pl.when(z == 1)
            def _():
                hop(k, h, z, facing).start()

            @pl.when(z != 3)
            def _():
                hop(k, h, z, pair).start()

            across(k, h, z).start()
        else:
            for d in range(1, nhi):
                hop(k, h, z, (z + d) % nhi).start()
            across(k, h, z).start()

    def relay(k, h, d):
        zz = order[d]
        hop(k, h, zz, z).wait_recv()
        if not line:
            across(k, h, zz).start()
            return
        if d == 1:
            @pl.when(z == 2)
            def _():
                hop(k, h, zz, pair).start()
        elif d == 2:
            @pl.when(z == 1)
            def _():
                hop(k, h, zz, facing).start()
        else:
            @pl.when(inner)
            def _():
                hop(k, h, zz, pair).start()

        if (k, h) in detour and d < 3:
            @pl.when(end if d == 2 else inner)
            def _():
                across(k, h, zz).start()
        else:
            across(k, h, zz).start()

    def pass_on(j):
        k, h = detour[j]
        gcopy(k, h, 1 - y, z, ys.at[h], gd.at[j], z * 2 + 1 - y).wait_recv()
        around(k, h).start()

    def multiply(k, h, acc):
        span = slice(spans[h].start, padded if h == last else spans[h].stop)
        for yy in range(2):
            for zz in range(nhi):
                at = (yy * nhi + zz) * rows
                feed[at:at + rows, spans[h]] = gath[k, yy, zz, :, spans[h]]
        f = feed[:, span]
        fh = f.astype(jnp.bfloat16)
        fl = (f - fh.astype(jnp.float32)).astype(jnp.bfloat16)
        both = jnp.concatenate([fh, fl], axis=0)
        big = jnp.dot(both, hi[k, span], preferred_element_type=jnp.float32)
        small = jnp.dot(fh, lo[k, span], preferred_element_type=jnp.float32)
        part = big[:group] + (big[group:] + small)
        return part if acc is None else acc + part

    @pl.when(q == 0)
    def _():
        with scope("cb"):
            for k in range(min(1, own)):
                convert(k)
        for h in parts:
            over_x(h)

    @pl.when(q == 1)
    def _():
        with scope("cb"):
            for k in range(min(2, own)):
                convert(k)


    acc = None
    for h in parts:
        for k in range(own):
            with scope(f"own{h}{k}"):
                own_piece(k, h)
    pieces = [(k, h) for h in parts for k in range(own)]
    with scope("cm"):
        for k in range(0, min(0 + 0, own)):
            convert(k)

    if line:
        @pl.when(z == 3)
        def _():
            for k, h in pieces:
                hop(k, h, z, pair).start()

        @pl.when(z == 2)
        def _():
            for k, h in pieces:
                hop(k, h, z, facing).start()

    with scope("cc"):
        for k in range(1, min(2, own)):
            @pl.when(q == 0)
            def _():
                convert(k)

        for k in range(2, own):
            convert(k)


    if line:
        pass

        for layer, lags in ((1, (12, -3, 0)), (2, (0, 1, 4))):
            @pl.when(z == layer)
            def _():
                for _, d, j in sorted((j + lags[d - 1], d, j) for j in range(len(pieces)) for d in range(1, nhi)):
                    with scope(f"i{d}_{j}"):
                        relay(*pieces[j], d)

        @pl.when(end)
        def _():
            for j in range(len(pieces)):
                with scope(f"e1_{j}"):
                    relay(*pieces[j], 1)
            for j in range(0):
                with scope(f"e2_{j}"):
                    relay(*pieces[j], 2)
    else:
        for k, h in pieces:
            for d in range(1, nhi):
                relay(k, h, d)

    def product(j, acc):
        k, h = pieces[j]
        with scope(f"w{h}{k}"):
            many(nhi - ((k, h) in detour), h, ys.at[h], fill(k, h)).wait_recv()
        with scope(f"q{h}{k}"):
            return multiply(k, h, acc)

    mirror_copy.wait()
    for h in parts:
        core_all(h).wait_send()
        pltpu.make_async_remote_copy(
            src_ref=sendb.at[:, :, :, spans[h]], dst_ref=landed.at[:, :, :, spans[h]],
            send_sem=xs.at[h], recv_sem=xr.at[h, 0, 0],
            device_id=(b, (x + 1) % nx * 2 + q), device_id_type=MESH).wait_send()

    steps = sorted((j + (0, 10, 12)[d - 1], d, j) for j in range(len(pieces)) for d in (2, 3))
    last3 = [n for n, s in enumerate(steps) if s[1] == 3]
    ready = 0
    at = 0
    for j in range(len(pieces)):
        stop = last3[j] + 1
        if line:
            @pl.when(end)
            def _():
                for _, d, i in steps[at:stop]:
                    with scope(f"e{d}_{i}"):
                        relay(*pieces[i], d)
        at = stop
        if 9 <= j < len(pieces) - 1:
            acc = product(ready, acc)
            ready += 1
    for j in range(ready, len(pieces)):
        acc = product(j, acc)

    deep = group // 4
    for yy in range(2):
        first = acc[2 * yy * deep:(2 * yy + 1) * deep]
        second = acc[(2 * yy + 1) * deep:(2 * yy + 2) * deep]
        sums = first[:, :ab] + second[:, :ab]
        diffs = first[:, ab:] - second[:, ab:]
        swapped = 0.5 * (sums - diffs)
        direct = 0.5 * (sums + diffs)
        for zz in range(nhi // 2):
            at = (zz * 2 + yy) * rows
            swp[0, at:at + rows] = direct[zz * rows:(zz + 1) * rows]
            swp[1, at:at + rows] = swapped[zz * rows:(zz + 1) * rows]
    for g in range(ncol):
        for i in range(own_pairs):
            p = g * own_pairs + i
            osend[g, i:i + 1, :] = swp[0, p:p + 1] + swp[1, pl.ds(mirror[p], 1), :]

    def ocopy(j):
        return pltpu.make_async_remote_copy(
            src_ref=osend.at[(c + j) % ncol], dst_ref=orecv.at[j - 1],
            send_sem=os_.at[0], recv_sem=or_.at[0],
            device_id=(b, (c + j) % ncol), device_id_type=MESH)

    for j in range(1, ncol):
        ocopy(j).start()
    with scope("sends2"):
        for h in parts:
            gone = len([j for j in detour if j[1] == h])
            many(own * nhi - gone, h, ys.at[h], gy.at[0, 0]).wait_send()
            if line:
                for layer, count in ((0, own), (1, 4 * own), (2, 5 * own), (3, 2 * own)):
                    @pl.when(z == layer)
                    def _():
                        many(count + gone, h, zs.at[h], gy.at[0, 0]).wait_send()
            else:
                many(own * (nhi - 1), h, zs.at[h], gy.at[0, 0]).wait_send()
    total = osend[c]
    with scope("owait"):
        every = pltpu.make_async_remote_copy(
            src_ref=orecv, dst_ref=orecv, send_sem=os_.at[0], recv_sem=or_.at[0],
            device_id=(b, (c + 1) % ncol), device_id_type=MESH)
        every.wait_recv()
    for j in range(1, ncol):
        total = total + orecv[j - 1]
    out_ref[...] = total
    every.wait_send()


def chunks(width):
    middle = width // 2 // 256 * 256
    return (slice(0, middle), slice(middle, width)) if middle else (slice(0, width),)


def body(nblk, ncol, amplitudes, integrals, block_ids, mirror):
    blocks_here, rows, width = amplitudes.shape
    _, ab, own, _ = integrals.shape
    pairs = mirror.shape[0]
    own_pairs = pairs // ncol
    padded = -(-width // 128) * 128
    nhi = nblk // 2
    nx = ncol // 2
    f32 = jnp.float32
    dma = pltpu.SemaphoreType.DMA
    parts = len(chunks(width))
    return pl.pallas_call(
        functools.partial(kernel, nblk, ncol),
        out_shape=pltpu.VMEM((own_pairs, ab), f32),
        in_specs=[pl.BlockSpec(memory_space=pl.ANY)] * 4,
        out_specs=pl.BlockSpec(memory_space=pltpu.VMEM),
        scratch_shapes=[
            tuple(pltpu.VMEM((blocks_here, rows, s.stop - s.start), f32) for s in chunks(width)),
            pltpu.VMEM((own, 2 * width, ab), f32),
            pltpu.VMEM((own, padded, 2 * ab), jnp.bfloat16),
            pltpu.VMEM((own, padded, 2 * ab), jnp.bfloat16),
            pltpu.VMEM((own, nx, rows, width), f32),
            pltpu.VMEM((own, nx, rows, width), f32),
            pltpu.VMEM((own, nx - 1, rows, width), f32),
            pltpu.VMEM((own, nx - 1, rows, width), f32),
            pltpu.VMEM((own, 2, nhi, rows, width), f32),
            pltpu.VMEM((2 * nhi * rows, padded), f32),
            pltpu.VMEM((2, pairs, ab), f32),
            pltpu.VMEM((ncol, own_pairs, ab), f32),
            pltpu.VMEM((ncol - 1, own_pairs, ab), f32),
            pltpu.SMEM(block_ids.shape, jnp.int32),
            pltpu.SMEM(mirror.shape, jnp.int32),
            dma((parts,)),
            dma((own,)),
            dma((2,)),
            dma((parts,)),
            dma((parts,)),
            dma((parts,)),
            dma((parts, own, nx - 1)),
            dma((parts,)),
            dma((parts,)),
            dma((parts, own, nhi - 1)),
            dma((1,)),
            dma((parts, own)),
            dma((1,)),
            dma((1,)),
        ],
        compiler_params=pltpu.CompilerParams(
            collective_id=0, has_side_effects=True, vmem_limit_bytes=60 * 1024 * 1024
        ),
    )(amplitudes, jnp.transpose(integrals, (2, 3, 0, 1)), block_ids, mirror)


def solution(mesh):
    in_specs = (P("col", "blk", None), P(None, "blk", "col", None), P(), P())
    out_specs = P("col", "blk")
    call = functools.partial(body, mesh.shape["blk"], mesh.shape["col"])
    return jax.shard_map(call, mesh=mesh, in_specs=in_specs, out_specs=out_specs, check_vma=False)
```

```python
import functools
from contextlib import nullcontext as scope

import jax
import jax.numpy as jnp
from jax import lax
from jax.experimental import pallas as pl
from jax.experimental.pallas import tpu as pltpu
from jax.sharding import PartitionSpec as P

MESH = pl.DeviceIdType.MESH


def kernel(
    nblk, ncol,
    amp_hbm, int_hbm, ids_hbm, mirror_hbm, out_ref,
    amp_v, int_v, hi, lo, core_out, core_in, sendb, landed, gath, feed, swp, osend, orecv, ids, mirror,
    amp_sem, int_sem, tab_sem, cr, xr, ss, gz, gy, os_, or_,
):
    blocks_here, rows, width = amp_hbm.shape
    own, _, ab = int_v.shape
    spans = chunks(width)
    parts = range(len(spans))
    last = parts[-1]
    padded = hi.shape[1]
    group = feed.shape[0]
    own_pairs = osend.shape[1]
    nhi = nblk // 2
    nx = ncol // 2
    b = lax.axis_index("blk")
    c = lax.axis_index("col")
    z = b // 2
    y = b % 2
    x = c // 2
    q = c % 2
    line = nhi == 4
    pair = z + 1 - 2 * (z % 2)
    facing = nhi - 1 - z
    cross = facing + 1 - 2 * (facing % 2)
    end = jnp.logical_or(z == 0, z == nhi - 1)
    inner = jnp.logical_not(end)
    if line:
        order = (z, jnp.where(end, pair, facing), jnp.where(end, cross, pair), jnp.where(end, facing, cross))
    else:
        order = tuple((z + nhi - d) % nhi for d in range(nhi))

    ids_copy = pltpu.make_async_copy(ids_hbm, ids, tab_sem.at[0])
    mirror_copy = pltpu.make_async_copy(mirror_hbm, mirror, tab_sem.at[1])
    ids_copy.start()
    amp_copies = []
    for h in parts:
        for i in range(4):
            at = pl.ds(blocks_here * i // 4, blocks_here * (i + 1) // 4 - blocks_here * i // 4)
            pltpu.make_async_copy(amp_hbm.at[at, :, spans[h]], amp_v[h].at[at], amp_sem.at[h]).start()
        amp_copies.append(pltpu.make_async_copy(amp_hbm.at[:, :, spans[h]], amp_v[h], amp_sem.at[h]))
    mirror_copy.start()
    barrier = pltpu.get_barrier_semaphore()

    def greet(target):
        pl.semaphore_signal(barrier, inc=1, device_id=target, device_id_type=MESH)

    with scope("barw"):
        for j in range(1, ncol):
            greet((b, (c + j) % ncol))
        greet((z * 2 + 1 - y, c))
        if line:
            greet((pair * 2 + y, c))

            @pl.when(inner)
            def _():
                greet((facing * 2 + y, c))

            @pl.when(z == 1)
            def _():
                greet((3 * 2 + y, c))

            @pl.when(z == 0)
            def _():
                greet((2 * 2 + y, c))

            pl.semaphore_wait(barrier, ncol + 2 - (z == 0).astype(jnp.int32) + (z == 2).astype(jnp.int32))
        else:
            for d in range(1, nhi):
                greet((order[d] * 2 + y, c))
            pl.semaphore_wait(barrier, ncol + nhi - 1)

    def core_copy(k, i, h):
        return pltpu.make_async_remote_copy(
            src_ref=core_out.at[k, i, :, spans[h]], dst_ref=core_in.at[k, i, :, spans[h]],
            send_sem=ss.at[h], recv_sem=cr.at[h],
            device_id=(b, x * 2 + 1 - q), device_id_type=MESH)

    def core_all(h):
        return pltpu.make_async_remote_copy(
            src_ref=core_out.at[:, :, :, spans[h]], dst_ref=core_in.at[:, :, :, spans[h]],
            send_sem=ss.at[h], recv_sem=cr.at[h],
            device_id=(b, x * 2 + 1 - q), device_id_type=MESH)

    def xcopy(k, i, h):
        return pltpu.make_async_remote_copy(
            src_ref=sendb.at[k, i - 1, :, spans[h]], dst_ref=landed.at[k, i - 1, :, spans[h]],
            send_sem=ss.at[h], recv_sem=xr.at[h, k, i - 1],
            device_id=(b, (x + i) % nx * 2 + 1 - q), device_id_type=MESH)

    def gcopy(k, h, yy, zz, send, recv, target):
        piece = gath.at[k, yy, zz, :, spans[h]]
        return pltpu.make_async_remote_copy(
            src_ref=piece, dst_ref=piece, send_sem=send, recv_sem=recv,
            device_id=(target, c), device_id_type=MESH)

    def across(k, h, zz):
        return gcopy(k, h, y, zz, ss.at[h], gy.at[h, k], z * 2 + 1 - y)

    def hop(k, h, zsrc, zdst):
        return gcopy(k, h, y, zsrc, ss.at[h], gz.at[h, k, (zsrc + nhi - zdst) % nhi - 1], zdst * 2 + y)

    def many(count, h, send, recv):
        piece = gath.reshape(own * nblk, rows, width).at[0:count, :, spans[h]]
        return pltpu.make_async_remote_copy(
            src_ref=piece, dst_ref=piece, send_sem=send, recv_sem=recv,
            device_id=(z * 2 + 1 - y, c), device_id_type=MESH)

    base = c * blocks_here

    def wanted(k, dest, h):
        here = ids[dest * own + k] - base
        ok = jnp.logical_and(here >= 0, here < blocks_here)
        at = jnp.minimum(jnp.maximum(here, 0), blocks_here - 1)
        return jnp.where(ok, amp_v[h][at], 0.0)

    def to_core(h):
        with scope(f"amp{h}"):
            amp_copies[h].wait()
        for k in range(own):
            for i in [*range(1, nx), 0]:
                dest = (x + i) % nx * 2 + q if i else x * 2 + 1 - q
                core_out[k, i, :, spans[h]] = wanted(k, dest, h)
                core_copy(k, i, h).start()

    def over_x(h):
        with scope(f"x{h}"):
            core_all(h).wait_recv()
            for k in range(own):
                for i in range(1, nx):
                    mine = wanted(k, (x + i) % nx * 2 + 1 - q, h)
                    sendb[k, i - 1, :, spans[h]] = mine + core_in[k, i, :, spans[h]]
                    xcopy(k, i, h).start()

    ids_copy.wait()
    to_core(0)

    @pl.when(q == 1)
    def _():
        over_x(0)

    for h in parts[1:]:
        to_core(h)
    int_copies = {}
    for k in range(own):
        cp = pltpu.make_async_copy(int_hbm.at[k], int_v.at[k].reshape(width, 2, ab), int_sem.at[k])
        cp.start()
        int_copies[k] = cp

    @pl.when(q == 1)
    def _():
        for h in parts[1:]:
            over_x(h)
    tail = (width // 128) * 128
    if padded > width:
        feed[:, tail:] = jnp.zeros((group, padded - tail), jnp.float32)

    def convert(k):
        int_copies[k].wait()
        whole = width // 16

        def split(at, count):
            for w in range(2):
                v = int_v[k, pl.ds(at * 2 + w, count, stride=2), :]
                h = v.astype(jnp.bfloat16)
                l = (v - h.astype(jnp.float32)).astype(jnp.bfloat16)
                if count < 16:
                    blank = jnp.zeros((16 - count, ab), jnp.bfloat16)
                    h = jnp.concatenate([h, blank], axis=0)
                    l = jnp.concatenate([l, blank], axis=0)
                hi[k, pl.ds(at, 16), w * ab:(w + 1) * ab] = h
                lo[k, pl.ds(at, 16), w * ab:(w + 1) * ab] = l

        def strip(i, carry):
            split(pl.multiple_of(i * 16, 16), 16)
            return carry

        lax.fori_loop(0, whole, strip, 0, unroll=4)
        done = whole * 16
        if width > done:
            split(done, width - done)
            done += 16
        if padded > done:
            hi[k, done:] = jnp.zeros((padded - done, 2 * ab), jnp.bfloat16)
            lo[k, done:] = jnp.zeros((padded - done, 2 * ab), jnp.bfloat16)

    def own_piece(k, h):
        total = wanted(k, c, h) + core_in[k, 0, :, spans[h]]
        for i in range(1, nx):
            xcopy(k, i, h).wait_recv()
            total = total + landed[k, i - 1, :, spans[h]]
        gath[k, y, z, :, spans[h]] = total
        if line:
            @pl.when(z == 3)
            def _():
                hop(k, h, z, 1).start()

            @pl.when(z == 2)
            def _():
                hop(k, h, z, 0).start()

            @pl.when(z == 1)
            def _():
                hop(k, h, z, facing).start()

            @pl.when(z != 3)
            def _():
                hop(k, h, z, pair).start()

            across(k, h, z).start()
        else:
            for d in range(1, nhi):
                hop(k, h, z, (z + d) % nhi).start()
            across(k, h, z).start()

    def relay(k, h, d):
        zz = order[d]
        hop(k, h, zz, z).wait_recv()
        if not line:
            across(k, h, zz).start()
            return
        if d == 1:
            @pl.when(z == 2)
            def _():
                hop(k, h, zz, pair).start()
        elif d == 2:
            @pl.when(z == 1)
            def _():
                hop(k, h, zz, facing).start()
        else:
            @pl.when(inner)
            def _():
                hop(k, h, zz, pair).start()

        across(k, h, zz).start()

    def multiply(k, h, acc):
        span = slice(spans[h].start, padded if h == last else spans[h].stop)
        for yy in range(2):
            for zz in range(nhi):
                at = (yy * nhi + zz) * rows
                feed[at:at + rows, spans[h]] = gath[k, yy, zz, :, spans[h]]
        f = feed[:, span]
        fh = f.astype(jnp.bfloat16)
        fl = (f - fh.astype(jnp.float32)).astype(jnp.bfloat16)
        both = jnp.concatenate([fh, fl], axis=0)
        big = jnp.dot(both, hi[k, span], preferred_element_type=jnp.float32)
        small = jnp.dot(fh, lo[k, span], preferred_element_type=jnp.float32)
        part = big[:group] + (big[group:] + small)
        return part if acc is None else acc + part

    @pl.when(q == 0)
    def _():
        with scope("cb"):
            for k in range(min(1, own)):
                convert(k)
        for h in parts:
            over_x(h)

    @pl.when(q == 1)
    def _():
        with scope("cb"):
            for k in range(min(2, own)):
                convert(k)


    acc = None
    for h in parts:
        for k in range(own):
            with scope(f"own{h}{k}"):
                own_piece(k, h)
    pieces = [(k, h) for h in parts for k in range(own)]
    with scope("cm"):
        for k in range(0, min(0 + 0, own)):
            convert(k)

    if line:
        @pl.when(z == 3)
        def _():
            for k, h in pieces:
                hop(k, h, z, pair).start()

        @pl.when(z == 2)
        def _():
            for k, h in pieces:
                hop(k, h, z, facing).start()

    with scope("cc"):
        for k in range(1, min(2, own)):
            @pl.when(q == 0)
            def _():
                convert(k)

        for k in range(2, own):
            convert(k)


    if line:
        pass

        for layer, lags in ((1, (12, -3, 0)), (2, (0, 1, 4))):
            @pl.when(z == layer)
            def _():
                for _, d, j in sorted((j + lags[d - 1], d, j) for j in range(len(pieces)) for d in range(1, nhi)):
                    with scope(f"i{d}_{j}"):
                        relay(*pieces[j], d)

        @pl.when(end)
        def _():
            for j in range(len(pieces)):
                with scope(f"e1_{j}"):
                    relay(*pieces[j], 1)
            for j in range(0):
                with scope(f"e2_{j}"):
                    relay(*pieces[j], 2)
    else:
        for k, h in pieces:
            for d in range(1, nhi):
                relay(k, h, d)

    def product(j, acc):
        k, h = pieces[j]
        with scope(f"w{h}{k}"):
            many(nhi, h, ss.at[h], gy.at[h, k]).wait_recv()
        with scope(f"q{h}{k}"):
            return multiply(k, h, acc)

    mirror_copy.wait()
    steps = sorted((j + (0, 10, 12)[d - 1], d, j) for j in range(len(pieces)) for d in (2, 3))
    last3 = [n for n, s in enumerate(steps) if s[1] == 3]
    ready = 0
    at = 0
    for j in range(len(pieces)):
        stop = last3[j] + 1
        if line:
            @pl.when(end)
            def _():
                for _, d, i in steps[at:stop]:
                    with scope(f"e{d}_{i}"):
                        relay(*pieces[i], d)
        at = stop
        if 9 <= j < len(pieces) - 1:
            acc = product(ready, acc)
            ready += 1
    for j in range(ready, len(pieces)):
        acc = product(j, acc)

    deep = group // 4
    for yy in range(2):
        first = acc[2 * yy * deep:(2 * yy + 1) * deep]
        second = acc[(2 * yy + 1) * deep:(2 * yy + 2) * deep]
        sums = first[:, :ab] + second[:, :ab]
        diffs = first[:, ab:] - second[:, ab:]
        swapped = 0.5 * (sums - diffs)
        direct = 0.5 * (sums + diffs)
        for zz in range(nhi // 2):
            at = (zz * 2 + yy) * rows
            swp[0, at:at + rows] = direct[zz * rows:(zz + 1) * rows]
            swp[1, at:at + rows] = swapped[zz * rows:(zz + 1) * rows]
    for g in range(ncol):
        for i in range(own_pairs):
            p = g * own_pairs + i
            osend[g, i:i + 1, :] = swp[0, p:p + 1] + swp[1, pl.ds(mirror[p], 1), :]

    def ocopy(j):
        return pltpu.make_async_remote_copy(
            src_ref=osend.at[(c + j) % ncol], dst_ref=orecv.at[j - 1],
            send_sem=os_.at[0], recv_sem=or_.at[0],
            device_id=(b, (c + j) % ncol), device_id_type=MESH)

    for j in range(1, ncol):
        ocopy(j).start()
    with scope("sends2"):
        def sent(count):
            for h in parts:
                for at in range(0, count, blocks_here):
                    some = amp_v[h].at[0:min(blocks_here, count - at)]
                    pltpu.make_async_copy(some, some, ss.at[h]).wait()

        local = own * (2 * nx - 1) + own * nhi
        if line:
            for layer, count in enumerate((own, 4 * own, 5 * own, 2 * own)):
                @pl.when(z == layer)
                def _():
                    sent(local + count)
        else:
            sent(local + own * (nhi - 1))
    total = osend[c]
    with scope("owait"):
        every = pltpu.make_async_remote_copy(
            src_ref=orecv, dst_ref=orecv, send_sem=os_.at[0], recv_sem=or_.at[0],
            device_id=(b, (c + 1) % ncol), device_id_type=MESH)
        every.wait_recv()
    for j in range(1, ncol):
        total = total + orecv[j - 1]
    out_ref[...] = total
    every.wait_send()


def chunks(width):
    middle = width // 2 // 256 * 256
    return (slice(0, middle), slice(middle, width)) if middle else (slice(0, width),)


def body(nblk, ncol, amplitudes, integrals, block_ids, mirror):
    blocks_here, rows, width = amplitudes.shape
    _, ab, own, _ = integrals.shape
    pairs = mirror.shape[0]
    own_pairs = pairs // ncol
    padded = -(-width // 128) * 128
    nhi = nblk // 2
    nx = ncol // 2
    f32 = jnp.float32
    dma = pltpu.SemaphoreType.DMA
    parts = len(chunks(width))
    return pl.pallas_call(
        functools.partial(kernel, nblk, ncol),
        out_shape=pltpu.VMEM((own_pairs, ab), f32),
        in_specs=[pl.BlockSpec(memory_space=pl.ANY)] * 4,
        out_specs=pl.BlockSpec(memory_space=pltpu.VMEM),
        scratch_shapes=[
            tuple(pltpu.VMEM((blocks_here, rows, s.stop - s.start), f32) for s in chunks(width)),
            pltpu.VMEM((own, 2 * width, ab), f32),
            pltpu.VMEM((own, padded, 2 * ab), jnp.bfloat16),
            pltpu.VMEM((own, padded, 2 * ab), jnp.bfloat16),
            pltpu.VMEM((own, nx, rows, width), f32),
            pltpu.VMEM((own, nx, rows, width), f32),
            pltpu.VMEM((own, nx - 1, rows, width), f32),
            pltpu.VMEM((own, nx - 1, rows, width), f32),
            pltpu.VMEM((own, 2, nhi, rows, width), f32),
            pltpu.VMEM((2 * nhi * rows, padded), f32),
            pltpu.VMEM((2, pairs, ab), f32),
            pltpu.VMEM((ncol, own_pairs, ab), f32),
            pltpu.VMEM((ncol - 1, own_pairs, ab), f32),
            pltpu.SMEM(block_ids.shape, jnp.int32),
            pltpu.SMEM(mirror.shape, jnp.int32),
            dma((parts,)),
            dma((own,)),
            dma((2,)),
            dma((parts,)),
            dma((parts, own, nx - 1)),
            dma((parts,)),
            dma((parts, own, nhi - 1)),
            dma((parts, own)),
            dma((1,)),
            dma((1,)),
        ],
        compiler_params=pltpu.CompilerParams(
            collective_id=0, has_side_effects=True, vmem_limit_bytes=60 * 1024 * 1024
        ),
    )(amplitudes, jnp.transpose(integrals, (2, 3, 0, 1)), block_ids, mirror)


def solution(mesh):
    in_specs = (P("col", "blk", None), P(None, "blk", "col", None), P(), P())
    out_specs = P("col", "blk")
    call = functools.partial(body, mesh.shape["blk"], mesh.shape["col"])
    return jax.shard_map(call, mesh=mesh, in_specs=in_specs, out_specs=out_specs, check_vma=False)
```

```python
import functools
from contextlib import nullcontext as scope

import jax
import jax.numpy as jnp
from jax import lax
from jax.experimental import pallas as pl
from jax.experimental.pallas import tpu as pltpu
from jax.sharding import PartitionSpec as P

MESH = pl.DeviceIdType.MESH


def kernel(
    nblk, ncol,
    amp_hbm, int_hbm, ids_hbm, mirror_hbm, out_ref,
    amp_v, int_v, hi, lo, core_out, core_in, sendb, landed, gath, feed, swp, osend, orecv, ids, mirror,
    amp_sem, int_sem, tab_sem, cs, cr, xs, xr, zs, ys, gz, gd, gy, os_, or_,
):
    blocks_here, rows, width = amp_hbm.shape
    own, _, ab = int_v.shape
    spans = chunks(width)
    parts = range(len(spans))
    last = parts[-1]
    padded = hi.shape[1]
    group = feed.shape[0]
    own_pairs = osend.shape[1]
    nhi = nblk // 2
    nx = ncol // 2
    b = lax.axis_index("blk")
    c = lax.axis_index("col")
    z = b // 2
    y = b % 2
    x = c // 2
    q = c % 2
    line = nhi == 4
    pair = z + 1 - 2 * (z % 2)
    facing = nhi - 1 - z
    cross = facing + 1 - 2 * (facing % 2)
    end = jnp.logical_or(z == 0, z == nhi - 1)
    inner = jnp.logical_not(end)
    if line:
        order = (z, jnp.where(end, pair, facing), jnp.where(end, cross, pair), jnp.where(end, facing, cross))
        detour = ()
    else:
        order = tuple((z + nhi - d) % nhi for d in range(nhi))
        detour = ()

    ids_copy = pltpu.make_async_copy(ids_hbm, ids, tab_sem.at[0])
    mirror_copy = pltpu.make_async_copy(mirror_hbm, mirror, tab_sem.at[1])
    ids_copy.start()
    amp_copies = []
    for h in parts:
        for i in range(4):
            at = pl.ds(blocks_here * i // 4, blocks_here * (i + 1) // 4 - blocks_here * i // 4)
            pltpu.make_async_copy(amp_hbm.at[at, :, spans[h]], amp_v[h].at[at], amp_sem.at[h]).start()
        amp_copies.append(pltpu.make_async_copy(amp_hbm.at[:, :, spans[h]], amp_v[h], amp_sem.at[h]))
    mirror_copy.start()
    barrier = pltpu.get_barrier_semaphore()

    def greet(target):
        pl.semaphore_signal(barrier, inc=1, device_id=target, device_id_type=MESH)

    with scope("barw"):
        for j in range(1, ncol):
            greet((b, (c + j) % ncol))
        greet((z * 2 + 1 - y, c))
        if line:
            greet((pair * 2 + y, c))

            @pl.when(inner)
            def _():
                greet((facing * 2 + y, c))

            @pl.when(z == 1)
            def _():
                greet((3 * 2 + y, c))

            @pl.when(z == 0)
            def _():
                greet((2 * 2 + y, c))

            pl.semaphore_wait(barrier, ncol + 2 - (z == 0).astype(jnp.int32) + (z == 2).astype(jnp.int32))
        else:
            for d in range(1, nhi):
                greet((order[d] * 2 + y, c))
            pl.semaphore_wait(barrier, ncol + nhi - 1)

    def core_copy(k, i, h):
        return pltpu.make_async_remote_copy(
            src_ref=core_out.at[k, i, :, spans[h]], dst_ref=core_in.at[k, i, :, spans[h]],
            send_sem=cs.at[h], recv_sem=cr.at[h],
            device_id=(b, x * 2 + 1 - q), device_id_type=MESH)

    def core_all(h):
        return pltpu.make_async_remote_copy(
            src_ref=core_out.at[:, :, :, spans[h]], dst_ref=core_in.at[:, :, :, spans[h]],
            send_sem=cs.at[h], recv_sem=cr.at[h],
            device_id=(b, x * 2 + 1 - q), device_id_type=MESH)

    def xcopy(k, i, h):
        return pltpu.make_async_remote_copy(
            src_ref=sendb.at[k, i - 1, :, spans[h]], dst_ref=landed.at[k, i - 1, :, spans[h]],
            send_sem=xs.at[h], recv_sem=xr.at[h, k, i - 1],
            device_id=(b, (x + i) % nx * 2 + 1 - q), device_id_type=MESH)

    def gcopy(k, h, yy, zz, send, recv, target):
        piece = gath.at[k, yy, zz, :, spans[h]]
        return pltpu.make_async_remote_copy(
            src_ref=piece, dst_ref=piece, send_sem=send, recv_sem=recv,
            device_id=(target, c), device_id_type=MESH)

    def fill(k, h):
        return gy.at[h, k]

    def across(k, h, zz):
        early = (k, h) in detour and zz is z
        recv = gd.at[detour.index((k, h))] if early else fill(k, h)
        return gcopy(k, h, y, zz, ys.at[h], recv, z * 2 + 1 - y)

    def hop(k, h, zsrc, zdst):
        return gcopy(k, h, y, zsrc, zs.at[h], gz.at[h, k, (zsrc + nhi - zdst) % nhi - 1], zdst * 2 + y)

    def around(k, h):
        return gcopy(k, h, 1 - y, z, zs.at[h], fill(k, h), pair * 2 + y)

    def many(count, h, send, recv):
        piece = gath.reshape(own * nblk, rows, width).at[0:count, :, spans[h]]
        return pltpu.make_async_remote_copy(
            src_ref=piece, dst_ref=piece, send_sem=send, recv_sem=recv,
            device_id=(z * 2 + 1 - y, c), device_id_type=MESH)

    base = c * blocks_here

    def wanted(k, dest, h):
        here = ids[dest * own + k] - base
        ok = jnp.logical_and(here >= 0, here < blocks_here)
        at = jnp.minimum(jnp.maximum(here, 0), blocks_here - 1)
        return jnp.where(ok, amp_v[h][at], 0.0)

    def to_core(h):
        with scope(f"amp{h}"):
            amp_copies[h].wait()
        for k in range(own):
            for i in [*range(1, nx), 0]:
                dest = (x + i) % nx * 2 + q if i else x * 2 + 1 - q
                core_out[k, i, :, spans[h]] = wanted(k, dest, h)
                core_copy(k, i, h).start()

    def over_x(h):
        with scope(f"x{h}"):
            core_all(h).wait_recv()
            for k in range(own):
                for i in range(1, nx):
                    mine = wanted(k, (x + i) % nx * 2 + 1 - q, h)
                    sendb[k, i - 1, :, spans[h]] = mine + core_in[k, i, :, spans[h]]
                    xcopy(k, i, h).start()

    ids_copy.wait()
    to_core(0)

    @pl.when(q == 1)
    def _():
        over_x(0)

    for h in parts[1:]:
        to_core(h)
    int_copies = {}
    for k in range(own):
        cp = pltpu.make_async_copy(int_hbm.at[k], int_v.at[k].reshape(width, 2, ab), int_sem.at[k])
        cp.start()
        int_copies[k] = cp

    @pl.when(q == 1)
    def _():
        for h in parts[1:]:
            over_x(h)
    tail = (width // 128) * 128
    if padded > width:
        feed[:, tail:] = jnp.zeros((group, padded - tail), jnp.float32)

    def convert(k):
        int_copies[k].wait()
        whole = width // 16

        def split(at, count):
            for w in range(2):
                v = int_v[k, pl.ds(at * 2 + w, count, stride=2), :]
                h = v.astype(jnp.bfloat16)
                l = (v - h.astype(jnp.float32)).astype(jnp.bfloat16)
                if count < 16:
                    blank = jnp.zeros((16 - count, ab), jnp.bfloat16)
                    h = jnp.concatenate([h, blank], axis=0)
                    l = jnp.concatenate([l, blank], axis=0)
                hi[k, pl.ds(at, 16), w * ab:(w + 1) * ab] = h
                lo[k, pl.ds(at, 16), w * ab:(w + 1) * ab] = l

        def strip(i, carry):
            split(pl.multiple_of(i * 16, 16), 16)
            return carry

        lax.fori_loop(0, whole, strip, 0, unroll=4)
        done = whole * 16
        if width > done:
            split(done, width - done)
            done += 16
        if padded > done:
            hi[k, done:] = jnp.zeros((padded - done, 2 * ab), jnp.bfloat16)
            lo[k, done:] = jnp.zeros((padded - done, 2 * ab), jnp.bfloat16)

    def own_piece(k, h):
        total = wanted(k, c, h) + core_in[k, 0, :, spans[h]]
        for i in range(1, nx):
            xcopy(k, i, h).wait_recv()
            total = total + landed[k, i - 1, :, spans[h]]
        gath[k, y, z, :, spans[h]] = total
        if line:
            @pl.when(z == 3)
            def _():
                hop(k, h, z, 1).start()

            @pl.when(z == 2)
            def _():
                hop(k, h, z, 0).start()

            @pl.when(z == 1)
            def _():
                hop(k, h, z, facing).start()

            @pl.when(z != 3)
            def _():
                hop(k, h, z, pair).start()

            across(k, h, z).start()
        else:
            for d in range(1, nhi):
                hop(k, h, z, (z + d) % nhi).start()
            across(k, h, z).start()

    def relay(k, h, d):
        zz = order[d]
        hop(k, h, zz, z).wait_recv()
        if not line:
            across(k, h, zz).start()
            return
        if d == 1:
            @pl.when(z == 2)
            def _():
                hop(k, h, zz, pair).start()
        elif d == 2:
            @pl.when(z == 1)
            def _():
                hop(k, h, zz, facing).start()
        else:
            @pl.when(inner)
            def _():
                hop(k, h, zz, pair).start()

        if (k, h) in detour and d < 3:
            @pl.when(end if d == 2 else inner)
            def _():
                across(k, h, zz).start()
        else:
            across(k, h, zz).start()

    def pass_on(j):
        k, h = detour[j]
        gcopy(k, h, 1 - y, z, ys.at[h], gd.at[j], z * 2 + 1 - y).wait_recv()
        around(k, h).start()

    def multiply(k, h, acc):
        span = slice(spans[h].start, padded if h == last else spans[h].stop)
        for yy in range(2):
            for zz in range(nhi):
                at = (yy * nhi + zz) * rows
                feed[at:at + rows, spans[h]] = gath[k, yy, zz, :, spans[h]]
        f = feed[:, span]
        fh = f.astype(jnp.bfloat16)
        fl = (f - fh.astype(jnp.float32)).astype(jnp.bfloat16)
        both = jnp.concatenate([fh, fl], axis=0)
        big = jnp.dot(both, hi[k, span], preferred_element_type=jnp.float32)
        small = jnp.dot(fh, lo[k, span], preferred_element_type=jnp.float32)
        part = big[:group] + (big[group:] + small)
        return part if acc is None else acc + part

    @pl.when(q == 0)
    def _():
        with scope("cb"):
            for k in range(min(1, own)):
                convert(k)
        for h in parts:
            over_x(h)

    @pl.when(q == 1)
    def _():
        with scope("cb"):
            for k in range(min(2, own)):
                convert(k)


    acc = None
    for h in parts:
        for k in range(own):
            with scope(f"own{h}{k}"):
                own_piece(k, h)
    pieces = [(k, h) for h in parts for k in range(own)]
    with scope("cm"):
        for k in range(0, min(0 + 0, own)):
            convert(k)

    if line:
        @pl.when(z == 3)
        def _():
            for k, h in pieces:
                hop(k, h, z, pair).start()

        @pl.when(z == 2)
        def _():
            for k, h in pieces:
                hop(k, h, z, facing).start()

    with scope("cc"):
        for k in range(1, min(2, own)):
            @pl.when(q == 0)
            def _():
                convert(k)

        for k in range(2, own):
            convert(k)


    if line:
        pass

        for layer, lags in ((1, (12, -3, 0)), (2, (0, 1, 4))):
            @pl.when(z == layer)
            def _():
                for _, d, j in sorted((j + lags[d - 1], d, j) for j in range(len(pieces)) for d in range(1, nhi)):
                    with scope(f"i{d}_{j}"):
                        relay(*pieces[j], d)

        @pl.when(end)
        def _():
            for j in range(len(pieces)):
                with scope(f"e1_{j}"):
                    relay(*pieces[j], 1)
            for j in range(0):
                with scope(f"e2_{j}"):
                    relay(*pieces[j], 2)
    else:
        for k, h in pieces:
            for d in range(1, nhi):
                relay(k, h, d)

    def product(j, acc):
        k, h = pieces[j]
        with scope(f"w{h}{k}"):
            many(nhi - ((k, h) in detour), h, ys.at[h], fill(k, h)).wait_recv()
        with scope(f"q{h}{k}"):
            return multiply(k, h, acc)

    mirror_copy.wait()
    for h in parts:
        core_all(h).wait_send()
        pltpu.make_async_remote_copy(
            src_ref=sendb.at[:, :, :, spans[h]], dst_ref=landed.at[:, :, :, spans[h]],
            send_sem=xs.at[h], recv_sem=xr.at[h, 0, 0],
            device_id=(b, (x + 1) % nx * 2 + q), device_id_type=MESH).wait_send()

    steps = sorted((j + (0, 10, 12)[d - 1], d, j) for j in range(len(pieces)) for d in (2, 3))
    last3 = [n for n, s in enumerate(steps) if s[1] == 3]
    ready = 0
    at = 0
    for j in range(len(pieces)):
        stop = last3[j] + 1
        if line:
            @pl.when(end)
            def _():
                for _, d, i in steps[at:stop]:
                    with scope(f"e{d}_{i}"):
                        relay(*pieces[i], d)
        at = stop
        if 10 <= j < len(pieces) - 1:
            acc = product(ready, acc)
            ready += 1
    for j in range(ready, len(pieces)):
        acc = product(j, acc)

    deep = group // 4
    for yy in range(2):
        first = acc[2 * yy * deep:(2 * yy + 1) * deep]
        second = acc[(2 * yy + 1) * deep:(2 * yy + 2) * deep]
        sums = first[:, :ab] + second[:, :ab]
        diffs = first[:, ab:] - second[:, ab:]
        swapped = 0.5 * (sums - diffs)
        direct = 0.5 * (sums + diffs)
        for zz in range(nhi // 2):
            at = (zz * 2 + yy) * rows
            swp[0, at:at + rows] = direct[zz * rows:(zz + 1) * rows]
            swp[1, at:at + rows] = swapped[zz * rows:(zz + 1) * rows]
    for g in range(ncol):
        for i in range(own_pairs):
            p = g * own_pairs + i
            osend[g, i:i + 1, :] = swp[0, p:p + 1] + swp[1, pl.ds(mirror[p], 1), :]

    def ocopy(j):
        return pltpu.make_async_remote_copy(
            src_ref=osend.at[(c + j) % ncol], dst_ref=orecv.at[j - 1],
            send_sem=os_.at[0], recv_sem=or_.at[0],
            device_id=(b, (c + j) % ncol), device_id_type=MESH)

    for j in range(1, ncol):
        ocopy(j).start()
    with scope("sends2"):
        for h in parts:
            gone = len([j for j in detour if j[1] == h])
            many(own * nhi - gone, h, ys.at[h], gy.at[0, 0]).wait_send()
            if line:
                for layer, count in ((0, own), (1, 4 * own), (2, 5 * own), (3, 2 * own)):
                    @pl.when(z == layer)
                    def _():
                        many(count + gone, h, zs.at[h], gy.at[0, 0]).wait_send()
            else:
                many(own * (nhi - 1), h, zs.at[h], gy.at[0, 0]).wait_send()
    total = osend[c]
    with scope("owait"):
        every = pltpu.make_async_remote_copy(
            src_ref=orecv, dst_ref=orecv, send_sem=os_.at[0], recv_sem=or_.at[0],
            device_id=(b, (c + 1) % ncol), device_id_type=MESH)
        every.wait_recv()
    for j in range(1, ncol):
        total = total + orecv[j - 1]
    out_ref[...] = total
    every.wait_send()


def chunks(width):
    middle = width // 2 // 256 * 256
    return (slice(0, middle), slice(middle, width)) if middle else (slice(0, width),)


def body(nblk, ncol, amplitudes, integrals, block_ids, mirror):
    blocks_here, rows, width = amplitudes.shape
    _, ab, own, _ = integrals.shape
    pairs = mirror.shape[0]
    own_pairs = pairs // ncol
    padded = -(-width // 128) * 128
    nhi = nblk // 2
    nx = ncol // 2
    f32 = jnp.float32
    dma = pltpu.SemaphoreType.DMA
    parts = len(chunks(width))
    return pl.pallas_call(
        functools.partial(kernel, nblk, ncol),
        out_shape=pltpu.VMEM((own_pairs, ab), f32),
        in_specs=[pl.BlockSpec(memory_space=pl.ANY)] * 4,
        out_specs=pl.BlockSpec(memory_space=pltpu.VMEM),
        scratch_shapes=[
            tuple(pltpu.VMEM((blocks_here, rows, s.stop - s.start), f32) for s in chunks(width)),
            pltpu.VMEM((own, 2 * width, ab), f32),
            pltpu.VMEM((own, padded, 2 * ab), jnp.bfloat16),
            pltpu.VMEM((own, padded, 2 * ab), jnp.bfloat16),
            pltpu.VMEM((own, nx, rows, width), f32),
            pltpu.VMEM((own, nx, rows, width), f32),
            pltpu.VMEM((own, nx - 1, rows, width), f32),
            pltpu.VMEM((own, nx - 1, rows, width), f32),
            pltpu.VMEM((own, 2, nhi, rows, width), f32),
            pltpu.VMEM((2 * nhi * rows, padded), f32),
            pltpu.VMEM((2, pairs, ab), f32),
            pltpu.VMEM((ncol, own_pairs, ab), f32),
            pltpu.VMEM((ncol - 1, own_pairs, ab), f32),
            pltpu.SMEM(block_ids.shape, jnp.int32),
            pltpu.SMEM(mirror.shape, jnp.int32),
            dma((parts,)),
            dma((own,)),
            dma((2,)),
            dma((parts,)),
            dma((parts,)),
            dma((parts,)),
            dma((parts, own, nx - 1)),
            dma((parts,)),
            dma((parts,)),
            dma((parts, own, nhi - 1)),
            dma((1,)),
            dma((parts, own)),
            dma((1,)),
            dma((1,)),
        ],
        compiler_params=pltpu.CompilerParams(
            collective_id=0, has_side_effects=True, vmem_limit_bytes=60 * 1024 * 1024
        ),
    )(amplitudes, jnp.transpose(integrals, (2, 3, 0, 1)), block_ids, mirror)


def solution(mesh):
    in_specs = (P("col", "blk", None), P(None, "blk", "col", None), P(), P())
    out_specs = P("col", "blk")
    call = functools.partial(body, mesh.shape["blk"], mesh.shape["col"])
    return jax.shard_map(call, mesh=mesh, in_specs=in_specs, out_specs=out_specs, check_vma=False)
```
